256 devices in a mesh: blk: 64 (over y_hi, z, x), rep: 2 (over core), layer: 2 (over y_lo).
Axes of the slice: x: 4, y: 4 (y_hi: 2, y_lo: 2; y = y_hi * 2 + y_lo), z: 8, core: 2. Of those that a mesh axis runs over, the one named last changes fastest.
Arguments:
- features: bfloat16 [3, 49152, 512], P(None, 'blk', 'rep'), may hold values from -6 to 6
- weights: bfloat16 [2, 512, 512], P('layer', None, 'rep'), may hold values from -0.25 to 0.25
- biases: bfloat16 [2, 512], P('layer', 'rep'), may hold values from -3 to 3
- tile_vals: bfloat16 [384, 24, 128, 128], P('blk'), may hold values from -0.25 to 0.25
- tile_cols: int32 [384, 24], P('blk'), may hold values from 0 to 383, as said below
- tile_counts: int32 [384], P('blk'), may hold values from 1 to 24, as said below
Outputs:
- layer_outputs: bfloat16 [2, 3, 49152, 512], P('layer', None, 'blk', 'rep')
The draws below stay inside these ranges and needn't reach their ends.
Inputs may be any that keep to these rules, and one draw needn't show every extreme that they name: tile_cols[b, k] is a column block of a blk index at most 2 places from the index that holds row block b, counted around the closed loop of blk indices: (b // 6 + d) mod (the number of blk indices), times 6, plus j, with -2 <= d <= 2 and 0 <= j < 6; the 24 entries of one row are distinct. The live tiles of row block b are its slots 0 to tile_counts[b] - 1; some row block has all 24 live.
All inputs are finite; a program needn't handle non-finite values.
Results may differ from the reference program's by a relative error of at most 0.0055.
Values may be sent and summed in bfloat16 or wider, within the bound.
A program may use at most 64 MiB of HBM per device.

```python
import jax
import jax.numpy as jnp
from jax import lax

F = 512
BLOCK = 128
RB_DEV = 6
TMAX = 24
REACH = 2
SNAPS = 3
NB = 384
NODES = 49152
N_BLK = 64


def draw_tile_cols(key, part):
    candidates = (2 * REACH + 1) * RB_DEV
    scores = jax.random.randint(key, (NB, candidates), 0, 1 << 20) * candidates + jnp.arange(candidates, dtype=jnp.int32)[None, :]
    chosen = jnp.argsort(scores, axis=1)[:, :TMAX].astype(jnp.int32)
    owners = (jnp.arange(NB, dtype=jnp.int32) // RB_DEV)[:, None]
    offsets = chosen // RB_DEV - REACH
    columns = (owners + offsets) % N_BLK * RB_DEV + chosen % RB_DEV
    return columns.astype(jnp.int32)


def draw_tile_counts(key, part):
    key_low, key_high, key_hot, key_peak = jax.random.split(jax.random.fold_in(key, 17), 4)
    lower_top = max(TMAX // 4, 1)
    upper_low = max(TMAX // 2, 1)
    light = jax.random.randint(key_low, (NB,), 1, lower_top + 1)
    heavy = jax.random.randint(key_high, (NB,), upper_low, TMAX + 1)
    marked = jax.random.randint(key_hot, (NB,), 0, 8) == 0
    counts = jnp.where(marked, heavy, light)
    peak_row = jax.random.randint(key_peak, (), 0, NB)
    counts = jnp.where(jnp.arange(NB, dtype=jnp.int32) == peak_row, TMAX, counts)
    return counts.astype(jnp.int32)


def level_of(stream_key, dims, cuts, least, high):
    loudness = 1.0
    for axis_at, shards_of in cuts:
        heights = jax.random.uniform(jax.random.fold_in(jax.random.fold_in(stream_key, 6), axis_at), (shards_of,), jnp.float32, least / len(cuts), high / len(cuts))
        loudness = loudness * jnp.repeat(jnp.exp(heights), dims[axis_at] // shards_of).reshape((-1,) + (1,) * (len(dims) - 1 - axis_at))
    return loudness


def bell_draw(key, dims, scale, reach, cuts=(), kind=jnp.bfloat16):
    factor_of = level_of(key, dims, cuts, -0.22, 0.18) if cuts else 1.0
    result = jax.random.normal(key, dims, jnp.float32) * scale * factor_of
    return jnp.minimum(jnp.maximum(result, -reach), reach).astype(kind)


def setup_inputs(seed: int = 0) -> dict:
    key_list = jax.random.split(jax.random.key(seed), 7)
    features = bell_draw(key_list[0], (SNAPS, NODES, F), 1.0, 6.0, ((1, 64), (2, 2)))
    weights = bell_draw(key_list[1], (2, F, F), F ** -0.5, 0.25, ((0, 2), (2, 2)))
    biases = bell_draw(key_list[2], (2, F), 0.5, 3.0, ((0, 2), (1, 2)))
    tile_vals = bell_draw(key_list[3], (NB, TMAX, BLOCK, BLOCK), (BLOCK * 4) ** -0.5, 0.25, ((0, 64),))
    tile_cols = draw_tile_cols(jax.random.fold_in(key_list[6], 71), 0)
    tile_counts = draw_tile_counts(jax.random.fold_in(key_list[6], 71), 0)
    return dict(features=features, weights=weights, biases=biases, tile_vals=tile_vals, tile_cols=tile_cols, tile_counts=tile_counts)


def aggregate(transformed, tile_vals, tile_cols, tile_counts):
    width = transformed.shape[1]
    blocks = transformed.reshape(NB, BLOCK, width)
    slot_ids = jnp.arange(TMAX, dtype=jnp.int32)

    def one_row(packed):
        values, columns, count = packed
        picked = blocks[columns.astype(jnp.int32)].astype(jnp.float32)
        picked = jnp.where((slot_ids < count.astype(jnp.int32))[:, None, None], picked, 0.0)
        return jnp.einsum("tij,tjf->if", values.astype(jnp.float32), picked, precision=lax.Precision.HIGHEST)

    summed = lax.map(one_row, (tile_vals, tile_cols, tile_counts))
    return summed.reshape(NODES, width)


def reference(features, weights, biases, tile_vals, tile_cols, tile_counts):
    transformed_first = jnp.concatenate(
        [jnp.dot(features[snap_index], weights[0], preferred_element_type=jnp.float32).astype(jnp.bfloat16) for snap_index in range(SNAPS)], axis=1)
    summed_first = aggregate(transformed_first, tile_vals, tile_cols, tile_counts)
    bias_first = jnp.tile(biases[0].astype(jnp.float32), SNAPS)
    hidden = jnp.maximum(summed_first + bias_first, 0.0).astype(jnp.bfloat16)
    hidden_list = [hidden[:, snap_index * F:(snap_index + 1) * F] for snap_index in range(SNAPS)]
    transformed_second = jnp.concatenate(
        [jnp.dot(hidden_list[snap_index], weights[1], preferred_element_type=jnp.float32).astype(jnp.bfloat16) for snap_index in range(SNAPS)], axis=1)
    summed_second = aggregate(transformed_second, tile_vals, tile_cols, tile_counts)
    bias_second = jnp.tile(biases[1].astype(jnp.float32), SNAPS)
    second = (summed_second + bias_second).astype(jnp.bfloat16)
    second_list = [second[:, snap_index * F:(snap_index + 1) * F] for snap_index in range(SNAPS)]
    return jnp.stack([jnp.stack(hidden_list), jnp.stack(second_list)])
```

```python
import jax
import jax.numpy as jnp
from jax import lax
from jax.experimental import pallas as pl
from jax.experimental.pallas import tpu as pltpu
from jax.sharding import PartitionSpec as P

BLOCK = 128
REACH = 2
SLABS = 2 * REACH + 1
HIGH_Y = 2
NEAR = 4
MESH = pl.DeviceIdType.MESH
BF16 = jnp.bfloat16
F32 = jnp.float32


def mm(a, b):
    return jnp.dot(a, b, preferred_element_type=F32)


def kernel(
    slot_of,
    bias,
    features,
    weights,
    tile_vals,
    out,
    tiles,
    dense,
    own_s,
    own_m,
    win_s,
    win_m,
    acc_s,
    acc_m,
    ax_s,
    ax_m,
    hid_s,
    hid_m,
    w_first,
    w_second,
    b_first,
    b_second,
    out_s,
    out_m,
    local_sem,
    send_sem,
    win_sem,
    ax_sem,
    side_send,
    w_sem,
    out_sem,
):
    blk = lax.axis_index("blk")
    rep = lax.axis_index("rep")
    layer = lax.axis_index("layer")
    n_blk = lax.axis_size("blk")
    per_y = n_blk // HIGH_Y
    role = lax.rem(layer + blk // per_y, 2)
    main_snap = 2 * role
    nodes = own_s.shape[1]
    half = nodes // 2
    row_blocks = nodes // BLOCK

    def along(offset):
        other = lax.rem(blk + offset + n_blk, n_blk)
        return {"blk": other, "rep": rep, "layer": lax.rem(role + other // per_y, 2)}

    def here(flip_rep, flip_layer):
        return {
            "blk": blk,
            "rep": 1 - rep if flip_rep else rep,
            "layer": 1 - layer if flip_layer else layer,
        }

    def remote(src, dst, send, recv, device):
        return pltpu.make_async_remote_copy(
            src_ref=src, dst_ref=dst, send_sem=send, recv_sem=recv,
            device_id=device, device_id_type=MESH,
        )

    share = pl.ds(pl.multiple_of(role * BLOCK, BLOCK), BLOCK)
    load_s = pltpu.make_async_copy(features.at[1, :, share], own_s.at[0], local_sem.at[0])
    load_m = pltpu.make_async_copy(features.at[main_snap], own_m.at[0], local_sem.at[1])
    n_tiles = tile_vals.shape[0]
    load_t = pltpu.make_async_copy(tile_vals, tiles.at[pl.ds(0, n_tiles)], local_sem.at[2])
    load_w0 = pltpu.make_async_copy(weights.at[0], w_first.at[rep], local_sem.at[3])
    load_w1 = pltpu.make_async_copy(weights.at[0], w_second, local_sem.at[3])
    load_s.start()
    load_m.start()
    load_t.start()
    spread = jnp.broadcast_to(bias[...], (16, bias.shape[1]))

    @pl.when(layer == 0)
    def _():
        load_w0.start()
        b_first[rep] = spread

    @pl.when(layer == 1)
    def _():
        load_w1.start()
        b_second[...] = spread

    tiles[n_tiles] = jnp.zeros((BLOCK, BLOCK), BF16)

    barrier = pltpu.get_barrier_semaphore()
    partners = [along(o) for o in (1, -1, NEAR, -NEAR)]
    partners += [here(True, False), here(False, True), here(True, True)]
    for partner in partners:
        pl.semaphore_signal(barrier, inc=1, device_id=partner, device_id_type=MESH)
    pl.semaphore_wait(barrier, len(partners))

    sent = []

    class Exchange:
        def __init__(self, which):
            def window(slot, chunk):
                rows = pl.ds((chunk % 2) * half, half)
                return (win_s if chunk < 2 else win_m).at[which, slot, rows]

            def own(chunk):
                rows = pl.ds((chunk % 2) * half, half)
                return (own_s if chunk < 2 else own_m).at[which, rows]

            def copy(src, slot, chunk, offset):
                made = remote(
                    src, window(slot, chunk), send_sem.at[len(sent)],
                    win_sem.at[which, slot, chunk], along(offset),
                )
                sent.append(made)
                return made

            self.right = [copy(own(c), 1, c, 1) for c in range(4)]
            self.left = [copy(own(c), 2, c, -1) for c in range(4)]
            self.right2 = {c: copy(window(1, c), 0, c, 1) for c in (0, 2)}
            self.left2 = {c: copy(window(2, c), 3, c, -1) for c in (1, 3)}
            self.right4 = {c: copy(window(3, c), 0, c, NEAR) for c in (1, 3)}
            self.left4 = {c: copy(window(0, c), 3, c, -NEAR) for c in (0, 2)}

        def pass_on(self, base):
            self.right[base].wait_recv()
            self.right2[base].start()
            self.left[base + 1].wait_recv()
            self.left2[base + 1].start()

        def near_ready(self, base):
            self.right[base + 1].wait_recv()
            self.left[base].wait_recv()

        def pass_far(self, base):
            self.right2[base].wait_recv()
            self.left4[base].start()
            self.left2[base + 1].wait_recv()
            self.right4[base + 1].start()

        def far_ready(self, base):
            self.left4[base].wait_recv()
            self.right4[base + 1].wait_recv()

    first = Exchange(0)
    second = Exchange(1)

    load_s.wait()
    first.right[0].start()
    first.left[1].start()
    first.right[1].start()
    first.left[0].start()
    load_m.wait()
    first.right[2].start()
    first.left[3].start()

    def send_first(index, device):
        return (
            remote(w_first.at[rep], w_first.at[rep], side_send.at[2 * index], w_sem.at[rep], device),
            remote(b_first.at[rep], b_first.at[rep], side_send.at[2 * index + 1], w_sem.at[2 + rep], device),
        )

    to_core = send_first(0, here(True, False))
    to_layer = send_first(1, here(False, True))
    to_both = send_first(2, here(True, True))
    back = (
        remote(w_second, w_second, side_send.at[0], w_sem.at[4], here(False, True)),
        remote(b_second, b_second, side_send.at[1], w_sem.at[5], here(False, True)),
    )
    from_rep = [
        (
            remote(w_first.at[c], w_first.at[c], side_send.at[0], w_sem.at[c], here(True, False)),
            remote(b_first.at[c], b_first.at[c], side_send.at[0], w_sem.at[2 + c], here(True, False)),
        )
        for c in range(2)
    ]

    @pl.when(layer == 0)
    def _():
        load_w0.wait()
        for made in to_core + to_layer + to_both:
            made.start()

    @pl.when(layer == 1)
    def _():
        load_w1.wait()
        for made in back:
            made.start()

    load_t.wait()

    def lay_row(b, carry):
        rows = pl.ds(pl.multiple_of(b * BLOCK, BLOCK), BLOCK)
        for d in range(SLABS):
            for j in range(row_blocks):
                cols = pl.ds(j * BLOCK, BLOCK)
                dense[d, rows, cols] = tiles[slot_of[b, d * row_blocks + j]]
        return carry

    lax.fori_loop(0, row_blocks, lay_row, 0)

    def slab(which, main, d):
        if d == REACH:
            return (own_m if main else own_s)[which]
        slot = d if d < REACH else d - 1
        return (win_m if main else win_s)[which, slot]

    def gather(which, main, slabs, start):
        acc = acc_m if main else acc_s
        total = mm(dense[slabs[0]], slab(which, main, slabs[0]))
        for d in slabs[1:]:
            total = total + mm(dense[d], slab(which, main, d))
        if start:
            acc[...] = total
        else:
            acc[...] += total

    def side(index, src, dst, recv, device):
        return remote(src, dst, side_send.at[index], recv, device)

    quarter = 2 * rep + role
    first.pass_on(0)
    first.right[3].start()
    first.left[2].start()
    gather(0, False, (2,), True)
    first.near_ready(0)
    gather(0, False, (1, 3), False)
    first.pass_far(0)
    gather(0, True, (2,), True)
    first.pass_on(2)
    first.far_ready(0)
    gather(0, False, (0, 4), False)
    ax_s[quarter] = acc_s[...].astype(BF16)
    ax_sent = [
        side(6 + i, ax_s.at[quarter], ax_s.at[quarter], ax_sem.at[quarter], device)
        for i, device in enumerate((here(False, True), here(True, True), here(True, False)))
    ]
    for made in ax_sent:
        made.start()
    first.near_ready(2)
    gather(0, True, (1, 3), False)

    @pl.when(layer == 0)
    def _():
        other = 1 - rep
        remote(w_first.at[other], w_first.at[other], side_send.at[0], w_sem.at[other], here(True, False)).wait_recv()
        remote(b_first.at[other], b_first.at[other], side_send.at[0], w_sem.at[2 + other], here(True, False)).wait_recv()
        for made in back:
            made.wait_recv()

    @pl.when(layer == 1)
    def _():
        for pair in from_rep:
            for made in pair:
                made.wait_recv()

    def hidden(parts, target):
        width = parts[0].shape[1]
        for c in range(2):
            total = mm(parts[0], w_first[c, pl.ds(0, width)])
            for i in range(1, len(parts)):
                total = total + mm(parts[i], w_first[c, pl.ds(i * width, width)])
            total = total + b_first[c, pl.ds(0, 1)].astype(F32)
            target[c] = jnp.maximum(total, 0.0).astype(BF16)

    def wait_quarter(q):
        side(9, ax_s.at[q], ax_s.at[q], ax_sem.at[q], here(True, False)).wait_recv()

    wait_quarter(2 * rep + 1 - role)
    wait_quarter(2 * (1 - rep) + role)
    wait_quarter(2 * (1 - rep) + 1 - role)
    hidden([ax_s[q] for q in range(4)], hid_s)
    cols = w_second.shape[0] // 2
    own_s[1] = (
        mm(hid_s[0], w_second[pl.ds(0, cols), share]) + mm(hid_s[1], w_second[pl.ds(cols, cols), share])
    ).astype(BF16)
    second.right[0].start()
    second.left[1].start()
    second.right[1].start()
    second.left[0].start()
    first.pass_far(2)

    keep_s = pltpu.make_async_copy(hid_s.at[rep], out.at[1], local_sem.at[4])

    @pl.when(layer == 0)
    def _():
        keep_s.start()

    first.far_ready(2)
    gather(0, True, (0, 4), False)
    ax_m[rep] = acc_m[...].astype(BF16)
    ax_main = side(9, ax_m.at[rep], ax_m.at[rep], ax_sem.at[4 + rep], here(True, False))
    ax_main.start()
    second.pass_on(0)
    gather(1, False, (2,), True)
    side(10, ax_m.at[1 - rep], ax_m.at[1 - rep], ax_sem.at[5 - rep], here(True, False)).wait_recv()
    hidden([ax_m[0], ax_m[1]], hid_m)
    own_m[1] = (
        mm(hid_m[0], w_second[pl.ds(0, cols)]) + mm(hid_m[1], w_second[pl.ds(cols, cols)])
    ).astype(BF16)
    second.right[2].start()
    second.left[3].start()
    second.right[3].start()
    second.left[2].start()

    keep_m = pltpu.make_async_copy(hid_m.at[rep], out.at[main_snap], local_sem.at[5])
    give_m = side(10, hid_m.at[rep], out.at[main_snap], out_sem.at[0], here(False, True))

    @pl.when(layer == 0)
    def _():
        keep_m.start()

    @pl.when(layer == 1)
    def _():
        give_m.start()

    second.near_ready(0)
    gather(1, False, (1, 3), False)
    second.pass_far(0)
    gather(1, True, (2,), True)
    second.pass_on(2)
    second.far_ready(0)
    gather(1, False, (0, 4), False)
    row = b_second[pl.ds(0, 1)].astype(F32)
    row_s = b_second[pl.ds(0, 1), share].astype(F32)
    out_s[...] = (acc_s[...] + row_s).astype(BF16)
    put_s = pltpu.make_async_copy(out_s, out.at[1, :, share], local_sem.at[4])
    push_s = side(11, out_s, out.at[1, :, share], out_sem.at[1], here(False, True))

    @pl.when(layer == 1)
    def _():
        put_s.start()

    @pl.when(layer == 0)
    def _():
        push_s.start()

    second.near_ready(2)
    gather(1, True, (1, 3), False)
    second.pass_far(2)
    second.far_ready(2)
    gather(1, True, (0, 4), False)
    out_m[...] = (acc_m[...] + row).astype(BF16)
    put_m = pltpu.make_async_copy(out_m, out.at[main_snap], local_sem.at[5])
    push_m = side(12, out_m, out.at[main_snap], out_sem.at[2], here(False, True))

    @pl.when(layer == 1)
    def _():
        put_m.start()
        put_s.wait()
        put_m.wait()
        other_cols = pl.ds(pl.multiple_of((1 - role) * BLOCK, BLOCK), BLOCK)
        side(11, out_s, out.at[1, :, other_cols], out_sem.at[1], here(False, True)).wait_recv()
        side(12, out_m, out.at[2 - main_snap], out_sem.at[2], here(False, True)).wait_recv()
        give_m.wait_send()
        for made in back:
            made.wait_send()

    @pl.when(layer == 0)
    def _():
        push_m.start()
        keep_s.wait()
        keep_m.wait()
        side(10, hid_m.at[rep], out.at[2 - main_snap], out_sem.at[0], here(False, True)).wait_recv()
        push_s.wait_send()
        push_m.wait_send()
        for made in to_core + to_layer + to_both:
            made.wait_send()

    ax_main.wait_send()
    for made in ax_sent:
        made.wait_send()
    for made in sent:
        made.wait_send()


def per_device(features, weights, biases, tile_vals, tile_cols, tile_counts):
    row_blocks, slots = tile_cols.shape
    snaps, nodes, width = features.shape
    n_tiles = row_blocks * slots
    blk = lax.axis_index("blk")
    n_blk = lax.axis_size("blk")
    places = jnp.arange(SLABS * row_blocks, dtype=jnp.int32)
    targets = (places // row_blocks + blk - REACH + n_blk) % n_blk * row_blocks + places % row_blocks
    slot_ids = lax.broadcasted_iota(jnp.int32, tile_cols.shape, 1)
    flat_ids = lax.broadcasted_iota(jnp.int32, tile_cols.shape, 0) * slots + slot_ids
    found = (tile_cols[:, :, None] == targets) & (slot_ids < tile_counts[:, None])[:, :, None]
    slot_of = n_tiles + jnp.sum(jnp.where(found, flat_ids[:, :, None] - n_tiles, 0), axis=1)

    result = pl.pallas_call(
        kernel,
        out_shape=jax.ShapeDtypeStruct(features.shape, BF16),
        in_specs=[
            pl.BlockSpec(memory_space=pltpu.SMEM),
            pl.BlockSpec(memory_space=pltpu.VMEM),
            pl.BlockSpec(memory_space=pl.ANY),
            pl.BlockSpec(memory_space=pl.ANY),
            pl.BlockSpec(memory_space=pl.ANY),
        ],
        out_specs=pl.BlockSpec(memory_space=pl.ANY),
        scratch_shapes=[
            pltpu.VMEM((n_tiles + 1, BLOCK, BLOCK), BF16),
            pltpu.VMEM((SLABS, nodes, nodes), BF16),
            pltpu.VMEM((2, nodes, BLOCK), BF16),
            pltpu.VMEM((2, nodes, width), BF16),
            pltpu.VMEM((2, 2 * REACH, nodes, BLOCK), BF16),
            pltpu.VMEM((2, 2 * REACH, nodes, width), BF16),
            pltpu.VMEM((nodes, BLOCK), F32),
            pltpu.VMEM((nodes, width), F32),
            pltpu.VMEM((4, nodes, BLOCK), BF16),
            pltpu.VMEM((2, nodes, width), BF16),
            pltpu.VMEM((2, nodes, width), BF16),
            pltpu.VMEM((2, nodes, width), BF16),
            pltpu.VMEM((2, 2 * width, width), BF16),
            pltpu.VMEM((2 * width, width), BF16),
            pltpu.VMEM((2, 16, width), BF16),
            pltpu.VMEM((16, width), BF16),
            pltpu.VMEM((nodes, BLOCK), BF16),
            pltpu.VMEM((nodes, width), BF16),
            pltpu.SemaphoreType.DMA((6,)),
            pltpu.SemaphoreType.DMA((32,)),
            pltpu.SemaphoreType.DMA((2, 2 * REACH, 4)),
            pltpu.SemaphoreType.DMA((6,)),
            pltpu.SemaphoreType.DMA((13,)),
            pltpu.SemaphoreType.DMA((6,)),
            pltpu.SemaphoreType.DMA((3,)),
        ],
        compiler_params=pltpu.CompilerParams(
            collective_id=0, has_side_effects=True, vmem_limit_bytes=48 * 1024 * 1024
        ),
    )(slot_of, biases, features, weights, tile_vals.reshape(n_tiles, BLOCK, BLOCK))
    return result[None]


def solution(mesh):
    return jax.shard_map(
        per_device,
        mesh=mesh,
        in_specs=(
            P(None, "blk", "rep"),
            P("layer", None, "rep"),
            P("layer", "rep"),
            P("blk", None, None, None),
            P("blk", None),
            P("blk"),
        ),
        out_specs=P("layer", None, "blk", "rep"),
        check_vma=False,
    )
```

```python
import jax
import jax.numpy as jnp
from jax import lax
from jax.experimental import pallas as pl
from jax.experimental.pallas import tpu as pltpu
from jax.sharding import PartitionSpec as P

BLOCK = 128
REACH = 2
SLABS = 2 * REACH + 1
HIGH_Y = 2
CHUNKS = 6
MESH = pl.DeviceIdType.MESH
BF16 = jnp.bfloat16
F32 = jnp.float32


def mm(a, b):
    return jnp.dot(a, b, preferred_element_type=F32)


def kernel(
    counts,
    bias,
    tile_cols,
    features,
    weights,
    tile_vals,
    out,
    table,
    slot_of,
    tiles,
    dense,
    own_s,
    own_m,
    own_p,
    win_s,
    win_m,
    win_p,
    acc_s,
    acc_m,
    ax_s,
    ax_m,
    hid_s,
    hid_m,
    w_first,
    w_second,
    b_first,
    b_second,
    out_p,
    local_sem,
    send_sem,
    win_sem,
    ax_sem,
    side_send,
    w_sem,
    out_sem,
):
    blk = lax.axis_index("blk")
    rep = lax.axis_index("rep")
    layer = lax.axis_index("layer")
    n_blk = lax.axis_size("blk")
    per_y = n_blk // HIGH_Y
    role = lax.rem(layer + blk // per_y, 2)
    main_snap = 2 * role
    nodes = own_s.shape[0]
    row_blocks = nodes // BLOCK
    n_tiles = tile_vals.shape[0]
    slots = n_tiles // row_blocks

    def along(offset):
        other = lax.rem(blk + offset + n_blk, n_blk)
        return {"blk": other, "rep": rep, "layer": lax.rem(role + other // per_y, 2)}

    def here(flip_rep, flip_layer):
        return {
            "blk": blk,
            "rep": 1 - rep if flip_rep else rep,
            "layer": 1 - layer if flip_layer else layer,
        }

    to_core, to_layer = here(True, False), here(False, True)

    def remote(src, dst, send, recv, device):
        return pltpu.make_async_remote_copy(
            src_ref=src, dst_ref=dst, send_sem=send, recv_sem=recv,
            device_id=device, device_id_type=MESH,
        )

    barrier = pltpu.get_barrier_semaphore()
    partners = [along(1), along(-1), to_core, to_layer]
    for partner in partners:
        pl.semaphore_signal(barrier, inc=1, device_id=partner, device_id_type=MESH)

    share = pl.ds(pl.multiple_of(role * BLOCK, BLOCK), BLOCK)
    load_s = pltpu.make_async_copy(features.at[1, :, share], own_s, local_sem.at[0])
    load_m = pltpu.make_async_copy(features.at[main_snap], own_m, local_sem.at[1])
    load_t = pltpu.make_async_copy(tile_vals, tiles.at[pl.ds(0, n_tiles)], local_sem.at[2])
    load_w0 = pltpu.make_async_copy(weights.at[0], w_first.at[rep], local_sem.at[3])
    load_w1 = pltpu.make_async_copy(weights.at[0], w_second, local_sem.at[3])
    load_s.start()
    load_m.start()
    load_t.start()
    spread = jnp.broadcast_to(bias[...], (16, bias.shape[1]))

    @pl.when(layer == 0)
    def _():
        load_w0.start()
        b_first[rep] = spread

    @pl.when(layer == 1)
    def _():
        load_w1.start()
        b_second[...] = spread

    tiles[n_tiles] = jnp.zeros((BLOCK, BLOCK), BF16)

    row_ids = lax.broadcasted_iota(jnp.int32, (row_blocks, slots), 0)
    slot_ids = lax.broadcasted_iota(jnp.int32, (row_blocks, slots), 1)
    live = jnp.zeros((row_blocks, slots), jnp.int32)
    for b in range(row_blocks):
        live = jnp.where(row_ids == b, counts[b], live)
    columns = jnp.where(slot_ids < live, tile_cols[...], -1)
    flat_ids = row_ids * slots + slot_ids - n_tiles
    lanes = lax.broadcasted_iota(jnp.int32, (row_blocks, BLOCK), 1)
    found = jnp.full((row_blocks, BLOCK), n_tiles, jnp.int32)
    for d in range(SLABS):
        first_block = lax.rem(blk + d - REACH + n_blk, n_blk) * row_blocks
        for j in range(row_blocks):
            hit = jnp.where(columns == first_block + j, flat_ids, 0)
            at = jnp.sum(hit, axis=1, keepdims=True)
            found = jnp.where(lanes == d * row_blocks + j, found + at, found)
    table[pl.ds(0, row_blocks)] = found

    pl.semaphore_wait(barrier, len(partners))

    sent = []

    class Exchange:
        def __init__(self, which, own, window):
            def copy(src, slot, chunk, offset):
                made = remote(
                    src, window(slot, chunk), send_sem.at[len(sent)],
                    win_sem.at[which, slot, chunk], along(offset),
                )
                sent.append(made)
                return made

            every = range(CHUNKS)
            self.right = [copy(own(c), 1, c, 1) for c in every]
            self.left = [copy(own(c), 2, c, -1) for c in every]
            self.right2 = [copy(window(1, c), 0, c, 1) for c in every]
            self.left2 = [copy(window(2, c), 3, c, -1) for c in every]

        def send(self, *chunks):
            for c in chunks:
                self.right[c].start()
                self.left[c].start()

        def pass_on(self, *chunks):
            for c in chunks:
                self.right[c].wait_recv()
                self.right2[c].start()
                self.left[c].wait_recv()
                self.left2[c].start()

        def far_ready(self, *chunks):
            for c in chunks:
                self.right2[c].wait_recv()
                self.left2[c].wait_recv()

    def half_rows(c):
        return pl.ds((c % 2) * (nodes // 2), nodes // 2)

    def main_rows(c):
        return pl.ds((c - 2) * (nodes // 4), nodes // 4)

    first = Exchange(
        0,
        lambda c: own_s.at[half_rows(c)] if c < 2 else own_m.at[main_rows(c)],
        lambda slot, c: win_s.at[slot, half_rows(c)] if c < 2 else win_m.at[slot, main_rows(c)],
    )
    second = Exchange(
        1,
        lambda c: own_p.at[c // 2, half_rows(c)],
        lambda slot, c: win_p.at[c // 2, slot, half_rows(c)],
    )

    load_s.wait()
    first.send(0, 1)
    load_m.wait()
    first.send(2)
    load_table = pltpu.make_async_copy(table, slot_of, local_sem.at[6])
    load_table.start()

    def side(index, src, dst, recv, device):
        return remote(src, dst, side_send.at[index], recv, device)

    def first_layer(index, c, device):
        return (
            side(index, w_first.at[c], w_first.at[c], w_sem.at[c], device),
            side(index + 1, b_first.at[c], b_first.at[c], w_sem.at[2 + c], device),
        )

    first_to_layer = first_layer(0, rep, to_layer)
    first_to_core = first_layer(2, rep, to_core)
    first_other = first_layer(2, 1 - rep, to_core)
    second_back = (
        side(0, w_second, w_second, w_sem.at[4], to_layer),
        side(1, b_second, b_second, w_sem.at[5], to_layer),
    )

    @pl.when(layer == 0)
    def _():
        load_w0.wait()
        for made in first_to_layer + first_to_core:
            made.start()

    @pl.when(layer == 1)
    def _():
        load_w1.wait()
        for made in second_back:
            made.start()

    load_table.wait()
    load_t.wait()

    def lay_row(b, carry):
        rows = pl.ds(pl.multiple_of(b * BLOCK, BLOCK), BLOCK)
        for d in range(SLABS):
            for j in range(row_blocks):
                cols = pl.ds(j * BLOCK, BLOCK)
                dense[d, rows, cols] = tiles[slot_of[b, d * row_blocks + j]]
        return carry

    lax.fori_loop(0, row_blocks, lay_row, 0)

    def gather(acc, slab, slabs, start):
        total = mm(dense[slabs[0]], slab(slabs[0]))
        for d in slabs[1:]:
            total = total + mm(dense[d], slab(d))
        if start:
            acc[...] = total
        else:
            acc[...] += total

    def part(own, win):
        return lambda d: own[...] if d == REACH else win[d if d < REACH else d - 1]

    part_s, part_m = part(own_s, win_s), part(own_m, win_m)
    parts = [part(own_p.at[p], win_p.at[p]) for p in range(3)]

    first.pass_on(0, 1)
    first.send(3, 4)
    gather(acc_s, part_s, (1, 2, 3), True)
    first.pass_on(2)
    first.send(5)
    first.far_ready(0, 1)
    gather(acc_s, part_s, (0, 4), False)
    quarter = 2 * rep + role
    ax_s[quarter] = acc_s[...].astype(BF16)
    across = side(4, ax_s.at[quarter], ax_s.at[quarter], ax_sem.at[quarter], to_layer)
    beside = side(5, ax_s.at[quarter], ax_s.at[quarter], ax_sem.at[quarter], to_core)
    across.start()
    beside.start()
    first.pass_on(3)

    @pl.when(layer == 1)
    def _():
        for made in first_layer(0, rep, to_layer):
            made.wait_recv()
        for made in first_to_core:
            made.start()

    gather(acc_m, part_m, (2,), True)
    first.pass_on(4)
    theirs = 2 * rep + 1 - role
    relayed = side(6, ax_s.at[theirs], ax_s.at[theirs], ax_sem.at[theirs], to_core)
    first.pass_on(5)
    relayed.wait_recv()
    relayed.start()
    gather(acc_m, part_m, (1, 3), False)
    for made in first_other:
        made.wait_recv()

    @pl.when(layer == 0)
    def _():
        for made in second_back:
            made.wait_recv()

    def hidden(pieces, target):
        width = pieces[0].shape[1]
        for c in range(2):
            total = mm(pieces[0], w_first[c, pl.ds(0, width)])
            for i in range(1, len(pieces)):
                total = total + mm(pieces[i], w_first[c, pl.ds(i * width, width)])
            total = total + b_first[c, pl.ds(0, 1)].astype(F32)
            target[c] = jnp.maximum(total, 0.0).astype(BF16)

    for q in (2 * (1 - rep) + role, 2 * (1 - rep) + 1 - role):
        side(6, ax_s.at[q], ax_s.at[q], ax_sem.at[q], to_core).wait_recv()
    hidden([ax_s[q] for q in range(4)], hid_s)
    cols = w_second.shape[0] // 2
    own_p[0] = (
        mm(hid_s[0], w_second[pl.ds(0, cols), share]) + mm(hid_s[1], w_second[pl.ds(cols, cols), share])
    ).astype(BF16)
    second.send(0, 1)
    first.far_ready(2, 3, 4, 5)
    gather(acc_m, part_m, (0, 4), False)
    ax_m[rep] = acc_m[...].astype(BF16)
    ax_main = side(7, ax_m.at[rep], ax_m.at[rep], ax_sem.at[4 + rep], to_core)
    ax_main.start()
    second.pass_on(0, 1)

    keep_s = pltpu.make_async_copy(hid_s.at[rep], out.at[1], local_sem.at[4])

    @pl.when(layer == 0)
    def _():
        keep_s.start()

    side(7, ax_m.at[1 - rep], ax_m.at[1 - rep], ax_sem.at[5 - rep], to_core).wait_recv()
    hidden([ax_m[0], ax_m[1]], hid_m)
    second_m = mm(hid_m[0], w_second[pl.ds(0, cols)]) + mm(hid_m[1], w_second[pl.ds(cols, cols)])
    own_p[1] = second_m[:, :BLOCK].astype(BF16)
    own_p[2] = second_m[:, BLOCK:].astype(BF16)
    second.send(2, 3, 4)

    keep_m = pltpu.make_async_copy(hid_m.at[rep], out.at[main_snap], local_sem.at[5])
    give_m = side(8, hid_m.at[rep], out.at[main_snap], out_sem.at[3], to_layer)

    @pl.when(layer == 0)
    def _():
        keep_m.start()

    @pl.when(layer == 1)
    def _():
        give_m.start()

    def piece_at(p, their_role):
        if p == 0:
            return out.at[1, :, pl.ds(pl.multiple_of(their_role * BLOCK, BLOCK), BLOCK)]
        return out.at[2 * their_role, :, pl.ds((p - 1) * BLOCK, BLOCK)]

    put = [pltpu.make_async_copy(out_p.at[p], piece_at(p, role), local_sem.at[7 + p]) for p in range(3)]
    push = [side(9 + p, out_p.at[p], piece_at(p, role), out_sem.at[p], to_layer) for p in range(3)]
    take = [side(9 + p, out_p.at[p], piece_at(p, 1 - role), out_sem.at[p], to_layer) for p in range(3)]

    def finish(p):
        gather(acc_s, parts[p], (0, 4), False)
        if p == 0:
            row = b_second[pl.ds(0, 1), share]
        else:
            row = b_second[pl.ds(0, 1), pl.ds((p - 1) * BLOCK, BLOCK)]
        out_p[p] = (acc_s[...] + row.astype(F32)).astype(BF16)

        @pl.when(layer == 1)
        def _():
            put[p].start()

        @pl.when(layer == 0)
        def _():
            push[p].start()

    gather(acc_s, parts[0], (1, 2, 3), True)
    second.far_ready(0, 1)
    finish(0)
    second.pass_on(2, 3)
    second.send(5)
    gather(acc_s, parts[1], (1, 2, 3), True)
    second.pass_on(4)
    second.far_ready(2, 3)
    finish(1)
    second.pass_on(5)
    gather(acc_s, parts[2], (1, 2, 3), True)
    second.far_ready(4, 5)
    finish(2)

    @pl.when(layer == 1)
    def _():
        for made in put:
            made.wait()
        for made in take:
            made.wait_recv()
        give_m.wait_send()
        for made in second_back + first_to_core:
            made.wait_send()

    @pl.when(layer == 0)
    def _():
        keep_s.wait()
        keep_m.wait()
        side(8, hid_m.at[rep], out.at[2 - main_snap], out_sem.at[3], to_layer).wait_recv()
        for made in push:
            made.wait_send()
        for made in first_to_layer + first_to_core:
            made.wait_send()

    for made in [ax_main, across, beside, relayed] + sent:
        made.wait_send()


def per_device(features, weights, biases, tile_vals, tile_cols, tile_counts):
    row_blocks, slots = tile_cols.shape
    snaps, nodes, width = features.shape
    n_tiles = row_blocks * slots
    tile_vals = tile_vals.reshape(n_tiles, BLOCK, BLOCK)
    features, weights, biases, tile_vals, tile_cols, tile_counts = (
        pltpu.with_memory_space_constraint(a, pltpu.HBM)
        for a in (features, weights, biases, tile_vals, tile_cols, tile_counts)
    )
    result = pl.pallas_call(
        kernel,
        out_shape=jax.ShapeDtypeStruct(features.shape, BF16),
        in_specs=[
            pl.BlockSpec(memory_space=pltpu.SMEM),
            pl.BlockSpec(memory_space=pltpu.VMEM),
            pl.BlockSpec(memory_space=pltpu.VMEM),
            pl.BlockSpec(memory_space=pl.ANY),
            pl.BlockSpec(memory_space=pl.ANY),
            pl.BlockSpec(memory_space=pl.ANY),
        ],
        out_specs=pl.BlockSpec(memory_space=pl.ANY),
        scratch_shapes=[
            pltpu.VMEM((8, BLOCK), jnp.int32),
            pltpu.SMEM((8, BLOCK), jnp.int32),
            pltpu.VMEM((n_tiles + 1, BLOCK, BLOCK), BF16),
            pltpu.VMEM((SLABS, nodes, nodes), BF16),
            pltpu.VMEM((nodes, BLOCK), BF16),
            pltpu.VMEM((nodes, width), BF16),
            pltpu.VMEM((3, nodes, BLOCK), BF16),
            pltpu.VMEM((2 * REACH, nodes, BLOCK), BF16),
            pltpu.VMEM((2 * REACH, nodes, width), BF16),
            pltpu.VMEM((3, 2 * REACH, nodes, BLOCK), BF16),
            pltpu.VMEM((nodes, BLOCK), F32),
            pltpu.VMEM((nodes, width), F32),
            pltpu.VMEM((4, nodes, BLOCK), BF16),
            pltpu.VMEM((2, nodes, width), BF16),
            pltpu.VMEM((2, nodes, width), BF16),
            pltpu.VMEM((2, nodes, width), BF16),
            pltpu.VMEM((2, 2 * width, width), BF16),
            pltpu.VMEM((2 * width, width), BF16),
            pltpu.VMEM((2, 16, width), BF16),
            pltpu.VMEM((16, width), BF16),
            pltpu.VMEM((3, nodes, BLOCK), BF16),
            pltpu.SemaphoreType.DMA((10,)),
            pltpu.SemaphoreType.DMA((8 * CHUNKS,)),
            pltpu.SemaphoreType.DMA((2, 2 * REACH, CHUNKS)),
            pltpu.SemaphoreType.DMA((6,)),
            pltpu.SemaphoreType.DMA((12,)),
            pltpu.SemaphoreType.DMA((6,)),
            pltpu.SemaphoreType.DMA((4,)),
        ],
        compiler_params=pltpu.CompilerParams(
            collective_id=0, has_side_effects=True, vmem_limit_bytes=48 * 1024 * 1024
        ),
    )(tile_counts, biases, tile_cols, features, weights, tile_vals)
    return result[None]


def solution(mesh):
    return jax.shard_map(
        per_device,
        mesh=mesh,
        in_specs=(
            P(None, "blk", "rep"),
            P("layer", None, "rep"),
            P("layer", "rep"),
            P("blk", None, None, None),
            P("blk", None),
            P("blk"),
        ),
        out_specs=P("layer", None, "blk", "rep"),
        check_vma=False,
    )
```

```python
import jax
import jax.numpy as jnp
from jax import lax
from jax.experimental import pallas as pl
from jax.experimental.pallas import tpu as pltpu
from jax.sharding import PartitionSpec as P

BLOCK = 128
REACH = 2
SLABS = 2 * REACH + 1
HIGH_Y = 2
CUTS = ((0, 512), (512, 256))
MAIN_ROWS = 256
MESH = pl.DeviceIdType.MESH
BF16 = jnp.bfloat16
F32 = jnp.float32


def mm(a, b):
    return jnp.dot(a, b, preferred_element_type=F32)


def kernel(
    counts,
    bias,
    tile_cols,
    features,
    weights,
    tile_vals,
    out,
    table,
    slot_of,
    tiles,
    dense,
    own_s,
    own_m,
    own_p,
    win_s,
    win_m,
    win_p,
    acc_s,
    acc_m,
    ax_s,
    ax_m,
    hid_s,
    hid_m,
    w_first,
    w_second,
    b_first,
    b_second,
    out_p,
    local_sem,
    send_sem,
    win_sem,
    ax_sem,
    side_send,
    w_sem,
    out_sem,
):
    blk = lax.axis_index("blk")
    rep = lax.axis_index("rep")
    layer = lax.axis_index("layer")
    n_blk = lax.axis_size("blk")
    per_y = n_blk // HIGH_Y
    role = lax.rem(layer + blk // per_y, 2)
    main_snap = 2 * role
    nodes = own_s.shape[0]
    row_blocks = nodes // BLOCK
    n_tiles = tile_vals.shape[0]
    slots = n_tiles // row_blocks

    def along(offset):
        other = lax.rem(blk + offset + n_blk, n_blk)
        return {"blk": other, "rep": rep, "layer": lax.rem(role + other // per_y, 2)}

    def here(flip_rep, flip_layer):
        return {
            "blk": blk,
            "rep": 1 - rep if flip_rep else rep,
            "layer": 1 - layer if flip_layer else layer,
        }

    to_core, to_layer = here(True, False), here(False, True)

    def remote(src, dst, send, recv, device):
        return pltpu.make_async_remote_copy(
            src_ref=src, dst_ref=dst, send_sem=send, recv_sem=recv,
            device_id=device, device_id_type=MESH,
        )

    barrier = pltpu.get_barrier_semaphore()
    partners = [along(1), along(-1), to_core, to_layer]
    for partner in partners:
        pl.semaphore_signal(barrier, inc=1, device_id=partner, device_id_type=MESH)

    share = pl.ds(pl.multiple_of(role * BLOCK, BLOCK), BLOCK)
    load_s = pltpu.make_async_copy(features.at[1, :, share], own_s, local_sem.at[0])
    load_m = pltpu.make_async_copy(features.at[main_snap], own_m, local_sem.at[1])
    load_t = pltpu.make_async_copy(tile_vals, tiles.at[pl.ds(0, n_tiles)], local_sem.at[2])
    load_w0 = pltpu.make_async_copy(weights.at[0], w_first.at[rep], local_sem.at[3])
    load_w1 = pltpu.make_async_copy(weights.at[0], w_second, local_sem.at[3])
    load_s.start()
    load_m.start()
    load_t.start()
    spread = jnp.broadcast_to(bias[...], (16, bias.shape[1]))

    @pl.when(layer == 0)
    def _():
        load_w0.start()
        b_first[rep] = spread

    @pl.when(layer == 1)
    def _():
        load_w1.start()
        b_second[...] = spread

    tiles[n_tiles] = jnp.zeros((BLOCK, BLOCK), BF16)

    row_ids = lax.broadcasted_iota(jnp.int32, (row_blocks, slots), 0)
    slot_ids = lax.broadcasted_iota(jnp.int32, (row_blocks, slots), 1)
    live = jnp.zeros((row_blocks, slots), jnp.int32)
    for b in range(row_blocks):
        live = jnp.where(row_ids == b, counts[b], live)
    columns = jnp.where(slot_ids < live, tile_cols[...], -1)
    flat_ids = row_ids * slots + slot_ids - n_tiles
    lanes = lax.broadcasted_iota(jnp.int32, (row_blocks, BLOCK), 1)
    found = jnp.full((row_blocks, BLOCK), n_tiles, jnp.int32)
    for d in range(SLABS):
        first_block = lax.rem(blk + d - REACH + n_blk, n_blk) * row_blocks
        for j in range(row_blocks):
            hit = jnp.where(columns == first_block + j, flat_ids, 0)
            at = jnp.sum(hit, axis=1, keepdims=True)
            found = jnp.where(lanes == d * row_blocks + j, found + at, found)
    table[pl.ds(0, row_blocks)] = found

    pl.semaphore_wait(barrier, len(partners))

    sent = []

    class Exchange:
        def __init__(self, which, chunks, own, window):
            def copy(src, slot, chunk, offset):
                made = remote(
                    src, window(slot, chunk), send_sem.at[len(sent)],
                    win_sem.at[which, slot, chunk], along(offset),
                )
                sent.append(made)
                return made

            every = range(chunks)
            self.right = [copy(own(c), 1, c, 1) for c in every]
            self.left = [copy(own(c), 2, c, -1) for c in every]
            self.right2 = [copy(window(1, c), 0, c, 1) for c in every]
            self.left2 = [copy(window(2, c), 3, c, -1) for c in every]

        def send(self, *chunks):
            for c in chunks:
                self.right[c].start()
                self.left[c].start()

        def pass_on(self, *chunks):
            for c in chunks:
                self.right[c].wait_recv()
                self.right2[c].start()
                self.left[c].wait_recv()
                self.left2[c].start()

        def far_ready(self, *chunks):
            for c in chunks:
                self.right2[c].wait_recv()
                self.left2[c].wait_recv()

    def cut_rows(c):
        return pl.ds(*CUTS[c % 2])

    def main_rows(c):
        return pl.ds((c - 2) * MAIN_ROWS, MAIN_ROWS)

    main_chunks = nodes // MAIN_ROWS
    first = Exchange(
        0,
        2 + main_chunks,
        lambda c: own_s.at[cut_rows(c)] if c < 2 else own_m.at[main_rows(c)],
        lambda slot, c: win_s.at[slot, cut_rows(c)] if c < 2 else win_m.at[slot, main_rows(c)],
    )
    second = Exchange(
        1,
        6,
        lambda c: own_p.at[c // 2, cut_rows(c)],
        lambda slot, c: win_p.at[c // 2, slot, cut_rows(c)],
    )

    load_s.wait()
    first.send(0, 1)
    load_m.wait()
    first.send(2)
    load_table = pltpu.make_async_copy(table, slot_of, local_sem.at[6])
    load_table.start()

    def side(index, src, dst, recv, device):
        return remote(src, dst, side_send.at[index], recv, device)

    def first_layer(index, c, device):
        return (
            side(index, w_first.at[c], w_first.at[c], w_sem.at[c], device),
            side(index + 1, b_first.at[c], b_first.at[c], w_sem.at[2 + c], device),
        )

    first_to_layer = first_layer(0, rep, to_layer)
    first_to_core = first_layer(2, rep, to_core)
    first_other = first_layer(2, 1 - rep, to_core)
    second_back = (
        side(0, w_second, w_second, w_sem.at[4], to_layer),
        side(1, b_second, b_second, w_sem.at[5], to_layer),
    )

    @pl.when(layer == 0)
    def _():
        load_w0.wait()
        for made in first_to_layer + first_to_core:
            made.start()

    @pl.when(layer == 1)
    def _():
        load_w1.wait()
        for made in second_back:
            made.start()

    load_table.wait()
    load_t.wait()

    def lay_row(b, carry):
        rows = pl.ds(pl.multiple_of(b * BLOCK, BLOCK), BLOCK)
        for d in range(SLABS):
            for j in range(row_blocks):
                cols = pl.ds(j * BLOCK, BLOCK)
                dense[d, rows, cols] = tiles[slot_of[b, d * row_blocks + j]]
        return carry

    lax.fori_loop(0, row_blocks, lay_row, 0)

    everything = pl.ds(0, nodes)

    def gather(acc, own, win, slabs, start=False, depth=everything, rows=everything):
        total = None
        for d in slabs:
            slab = own[depth] if d == REACH else win[d if d < REACH else d - 1, depth]
            product = mm(dense[d, rows, depth], slab)
            total = product if total is None else total + product
        if start:
            acc[rows] = total
        else:
            acc[rows] += total

    near, far = (1, 3), (0, 4)
    first.pass_on(0, 1)
    first.send(3)
    gather(acc_s, own_s, win_s, (2,) + near, True)
    first.pass_on(2)
    first.send(4)
    first.far_ready(0, 1)
    gather(acc_s, own_s, win_s, far)
    quarter = 2 * rep + role
    ax_s[quarter] = acc_s[...].astype(BF16)
    across = side(4, ax_s.at[quarter], ax_s.at[quarter], ax_sem.at[quarter], to_layer)
    beside = side(5, ax_s.at[quarter], ax_s.at[quarter], ax_sem.at[quarter], to_core)
    across.start()
    beside.start()
    first.pass_on(3)

    @pl.when(layer == 1)
    def _():
        for made in first_to_layer:
            made.wait_recv()
        for made in first_to_core:
            made.start()

    gather(acc_m, own_m, win_m, (2,), True)
    theirs = 2 * rep + 1 - role
    relayed = side(6, ax_s.at[theirs], ax_s.at[theirs], ax_sem.at[theirs], to_core)
    relayed.wait_recv()
    relayed.start()
    first.pass_on(4)
    for made in first_other:
        made.wait_recv()

    @pl.when(layer == 0)
    def _():
        for made in second_back:
            made.wait_recv()

    def hidden(pieces, target, rows):
        width = pieces[0].shape[1]
        for c in range(2):
            total = mm(pieces[0][rows], w_first[c, pl.ds(0, width)])
            for i in range(1, len(pieces)):
                total = total + mm(pieces[i][rows], w_first[c, pl.ds(i * width, width)])
            total = total + b_first[c, pl.ds(0, 1)].astype(F32)
            target[c, rows] = jnp.maximum(total, 0.0).astype(BF16)

    cols = w_second.shape[0] // 2
    quarters = [ax_s.at[q] for q in range(4)]
    for q in (2 * (1 - rep) + role, 2 * (1 - rep) + 1 - role):
        side(6, ax_s.at[q], ax_s.at[q], ax_sem.at[q], to_core).wait_recv()
    for c in range(2):
        rows = cut_rows(c)
        hidden(quarters, hid_s, rows)
        own_p[0, rows] = (
            mm(hid_s[0, rows], w_second[pl.ds(0, cols), share])
            + mm(hid_s[1, rows], w_second[pl.ds(cols, cols), share])
        ).astype(BF16)
        second.send(c)

    gather(acc_m, own_m, win_m, near)
    for c in range(2, 1 + main_chunks):
        first.far_ready(c)
        gather(acc_m, own_m, win_m, far, depth=main_rows(c))
    first.far_ready(1 + main_chunks)
    ax_main = []
    for c in range(2):
        rows = cut_rows(c)
        gather(acc_m, own_m, win_m, far, depth=main_rows(1 + main_chunks), rows=rows)
        ax_m[rep, rows] = acc_m[rows].astype(BF16)
        mine = ax_m.at[rep, rows]
        ax_main.append(side(7 + c, mine, mine, ax_sem.at[4 + 2 * rep + c], to_core))
        ax_main[c].start()

    keep_s = pltpu.make_async_copy(hid_s.at[rep], out.at[1], local_sem.at[4])

    @pl.when(layer == 0)
    def _():
        keep_s.start()

    for c in range(2):
        second.pass_on(c)
        rows = cut_rows(c)
        other = ax_m.at[1 - rep, rows]
        side(7 + c, other, other, ax_sem.at[6 - 2 * rep + c], to_core).wait_recv()
        hidden([ax_m.at[0], ax_m.at[1]], hid_m, rows)
        second_m = (
            mm(hid_m[0, rows], w_second[pl.ds(0, cols)]) + mm(hid_m[1, rows], w_second[pl.ds(cols, cols)])
        ).astype(BF16)
        own_p[1, rows] = second_m[:, :BLOCK]
        own_p[2, rows] = second_m[:, BLOCK:]
        second.send(2 + c)
    second.send(4)

    keep_m = pltpu.make_async_copy(hid_m.at[rep], out.at[main_snap], local_sem.at[5])
    give_m = side(9, hid_m.at[rep], out.at[main_snap], out_sem.at[6], to_layer)

    @pl.when(layer == 0)
    def _():
        keep_m.start()

    @pl.when(layer == 1)
    def _():
        give_m.start()

    def piece_at(p, rows, their_role):
        if p == 0:
            return out.at[1, rows, pl.ds(pl.multiple_of(their_role * BLOCK, BLOCK), BLOCK)]
        return out.at[2 * their_role, rows, pl.ds((p - 1) * BLOCK, BLOCK)]

    put, push, take = [], [], []
    for p in range(3):
        for c in range(2):
            i, src = 2 * p + c, out_p.at[p, cut_rows(c)]
            mine, other = piece_at(p, cut_rows(c), role), piece_at(p, cut_rows(c), 1 - role)
            put.append(pltpu.make_async_copy(src, mine, local_sem.at[7 + i]))
            push.append(side(10 + i, src, mine, out_sem.at[i], to_layer))
            take.append(side(10 + i, src, other, out_sem.at[i], to_layer))

    def finish(p):
        own, win = own_p.at[p], win_p.at[p]
        second.far_ready(2 * p)
        gather(acc_s, own, win, far, depth=cut_rows(0))
        second.far_ready(2 * p + 1)
        if p == 0:
            row = b_second[pl.ds(0, 1), share]
        else:
            row = b_second[pl.ds(0, 1), pl.ds((p - 1) * BLOCK, BLOCK)]
        for c in range(2):
            rows = cut_rows(c)
            gather(acc_s, own, win, far, depth=cut_rows(1), rows=rows)
            out_p[p, rows] = (acc_s[rows] + row.astype(F32)).astype(BF16)

            @pl.when(layer == 1)
            def _():
                put[2 * p + c].start()

            @pl.when(layer == 0)
            def _():
                push[2 * p + c].start()

    gather(acc_s, own_p.at[0], win_p.at[0], (2,) + near, True)
    finish(0)
    second.pass_on(2, 3)
    second.send(5)
    gather(acc_s, own_p.at[1], win_p.at[1], (2,) + near, True)
    second.pass_on(4)
    finish(1)
    second.pass_on(5)
    gather(acc_s, own_p.at[2], win_p.at[2], (2,) + near, True)
    finish(2)

    @pl.when(layer == 1)
    def _():
        for made in put:
            made.wait()
        for made in take:
            made.wait_recv()
        give_m.wait_send()
        for made in second_back + first_to_core:
            made.wait_send()

    @pl.when(layer == 0)
    def _():
        keep_s.wait()
        keep_m.wait()
        side(9, hid_m.at[rep], out.at[2 - main_snap], out_sem.at[6], to_layer).wait_recv()
        for made in push:
            made.wait_send()
        for made in first_to_layer + first_to_core:
            made.wait_send()

    for made in ax_main + [across, beside, relayed] + sent:
        made.wait_send()


def per_device(features, weights, biases, tile_vals, tile_cols, tile_counts):
    row_blocks, slots = tile_cols.shape
    snaps, nodes, width = features.shape
    n_tiles = row_blocks * slots
    tile_vals = tile_vals.reshape(n_tiles, BLOCK, BLOCK)
    features, weights, biases, tile_vals, tile_cols, tile_counts = (
        pltpu.with_memory_space_constraint(a, pltpu.HBM)
        for a in (features, weights, biases, tile_vals, tile_cols, tile_counts)
    )
    result = pl.pallas_call(
        kernel,
        out_shape=jax.ShapeDtypeStruct(features.shape, BF16),
        in_specs=[
            pl.BlockSpec(memory_space=pltpu.SMEM),
            pl.BlockSpec(memory_space=pltpu.VMEM),
            pl.BlockSpec(memory_space=pltpu.VMEM),
            pl.BlockSpec(memory_space=pl.ANY),
            pl.BlockSpec(memory_space=pl.ANY),
            pl.BlockSpec(memory_space=pl.ANY),
        ],
        out_specs=pl.BlockSpec(memory_space=pl.ANY),
        scratch_shapes=[
            pltpu.VMEM((8, BLOCK), jnp.int32),
            pltpu.SMEM((8, BLOCK), jnp.int32),
            pltpu.VMEM((n_tiles + 1, BLOCK, BLOCK), BF16),
            pltpu.VMEM((SLABS, nodes, nodes), BF16),
            pltpu.VMEM((nodes, BLOCK), BF16),
            pltpu.VMEM((nodes, width), BF16),
            pltpu.VMEM((3, nodes, BLOCK), BF16),
            pltpu.VMEM((2 * REACH, nodes, BLOCK), BF16),
            pltpu.VMEM((2 * REACH, nodes, width), BF16),
            pltpu.VMEM((3, 2 * REACH, nodes, BLOCK), BF16),
            pltpu.VMEM((nodes, BLOCK), F32),
            pltpu.VMEM((nodes, width), F32),
            pltpu.VMEM((4, nodes, BLOCK), BF16),
            pltpu.VMEM((2, nodes, width), BF16),
            pltpu.VMEM((2, nodes, width), BF16),
            pltpu.VMEM((2, nodes, width), BF16),
            pltpu.VMEM((2, 2 * width, width), BF16),
            pltpu.VMEM((2 * width, width), BF16),
            pltpu.VMEM((2, 16, width), BF16),
            pltpu.VMEM((16, width), BF16),
            pltpu.VMEM((3, nodes, BLOCK), BF16),
            pltpu.SemaphoreType.DMA((13,)),
            pltpu.SemaphoreType.DMA((48,)),
            pltpu.SemaphoreType.DMA((2, 2 * REACH, 6)),
            pltpu.SemaphoreType.DMA((8,)),
            pltpu.SemaphoreType.DMA((16,)),
            pltpu.SemaphoreType.DMA((6,)),
            pltpu.SemaphoreType.DMA((7,)),
        ],
        compiler_params=pltpu.CompilerParams(
            collective_id=0, has_side_effects=True, vmem_limit_bytes=48 * 1024 * 1024
        ),
    )(tile_counts, biases, tile_cols, features, weights, tile_vals)
    return result[None]


def solution(mesh):
    return jax.shard_map(
        per_device,
        mesh=mesh,
        in_specs=(
            P(None, "blk", "rep"),
            P("layer", None, "rep"),
            P("layer", "rep"),
            P("blk", None, None, None),
            P("blk", None),
            P("blk"),
        ),
        out_specs=P("layer", None, "blk", "rep"),
        check_vma=False,
    )
```
